32 devices in a mesh: space: 16 (over z, y, x), src: 2 (over core).
Axes of the slice: x: 2, y: 2, z: 4, core: 2. Of those that a mesh axis runs over, the one named last changes fastest.
Arguments:
- rhs: float32 [12288, 1024], P('space', 'src'), may hold values from -18 to 18
- diag_blocks: bfloat16 [48, 256, 256], P('space', 'src'), may hold values from -0.5 to 5.5
- couple_blocks: bfloat16 [48, 2, 256, 256], P('space', None, 'src'), may hold values from -0.1875 to 0.1875
- halo_weight: bfloat16 [32, 256, 128], P('space', 'src'), may hold values from -0.25 to 0.25
- neighbours: int32 [48, 2], P('space'), may hold values from 0 to 2
- boundary: int32 [32, 128], P('space'), may hold values from 0 to 767
Outputs:
- solution: float32 [12288, 1024], P('space', 'src')
- misfit: float32 [1024], P('src')
The draws below stay inside these ranges and needn't reach their ends.
All inputs are finite; a program needn't handle non-finite values.
Results may differ from the reference program's by a relative error of at most 0.0032.
Values may be sent and summed in bfloat16 or wider, within the bound.
A program may use at most 64 MiB of HBM per device.

```python
import jax
import jax.numpy as jnp
from jax import lax

EDGE_AGG = 256
HALO = 128
NBR = 2
SWEEPS = 4
AGG_DEV = 3
SRC_DEV = 512
EDGES = 12288
AGGS = 48
SOURCES = 1024
N_SPACE = 16
N_SRC = 2


def draw_rhs(key, part):
    ramp = 1.0 + 2.0 * jnp.arange(EDGES, dtype=jnp.float32) / EDGES
    base = jnp.clip(jax.random.normal(key, (EDGES, SOURCES), jnp.float32), -6.0, 6.0)
    return base * ramp[:, None]


def draw_diag_blocks(key, part):
    first, second = jax.random.split(key)
    noise = jnp.clip(jax.random.normal(first, (AGGS, EDGE_AGG, EDGE_AGG), jnp.float32), -6.0, 6.0)
    noise = jnp.clip(noise / jnp.sqrt(jnp.float32(EDGE_AGG)), -0.5, 0.5)
    shifts = jax.random.uniform(second, (AGGS, EDGE_AGG, 1), jnp.float32, 3.0, 5.0)
    identity = jnp.eye(EDGE_AGG, dtype=jnp.float32)[None]
    return (noise + identity * shifts).astype(jnp.bfloat16)


def touch_ends(result, stream_key, smallest, largest):
    index_at = [jax.random.randint(jax.random.fold_in(stream_key, axis), (), 0, length) for axis, length in enumerate(result.shape)]
    main_axis = result.shape.index(max(result.shape))
    beside = index_at[:main_axis] + [(index_at[main_axis] + 1) % result.shape[main_axis]] + index_at[main_axis + 1:]
    return result.at[tuple(index_at)].set(smallest).at[tuple(beside)].set(largest)


def levels(rng, dims, cuts, low, top_value):
    loudness = 1.0
    for axis_at, blocks in cuts:
        heights = jax.random.uniform(jax.random.fold_in(jax.random.fold_in(rng, 6), axis_at), (blocks,), jnp.float32, low / len(cuts), top_value / len(cuts))
        loudness = loudness * jnp.repeat(jnp.exp(heights), dims[axis_at] // blocks).reshape((-1,) + (1,) * (len(dims) - 1 - axis_at))
    return loudness


def scatter_about(key, extent, spread, bound, pieces=(), kind=jnp.bfloat16):
    loudness = levels(key, extent, pieces, -0.22, 0.18) if pieces else 1.0
    result = jax.random.normal(key, extent, jnp.float32) * spread * loudness
    return jnp.minimum(jnp.maximum(result, -bound), bound).astype(kind)


def setup_inputs(seed: int = 0) -> dict:
    streams_of = jax.random.split(jax.random.key(seed), 7)
    rhs = draw_rhs(jax.random.fold_in(streams_of[6], 71), 0)
    diag_blocks = draw_diag_blocks(jax.random.fold_in(streams_of[6], 71), 0)
    couple_blocks = scatter_about(streams_of[2], (AGGS, NBR, EDGE_AGG, EDGE_AGG), (4 * EDGE_AGG) ** -0.5, 0.1875, ((0, 16), (2, 2)))
    halo_weight = scatter_about(streams_of[3], (2 * N_SPACE, EDGE_AGG, HALO), (4 * HALO) ** -0.5, 0.25, ((0, 16), (1, 2)))
    neighbours = touch_ends(jax.random.randint(streams_of[4], (AGGS, NBR), 0, AGG_DEV), jax.random.fold_in(streams_of[4], 1), 0, AGG_DEV - 1).astype(jnp.int32)
    boundary = touch_ends(jax.random.randint(streams_of[5], (2 * N_SPACE, HALO), 0, AGG_DEV * EDGE_AGG), jax.random.fold_in(streams_of[5], 1), 0, (AGG_DEV * EDGE_AGG) - 1).astype(jnp.int32)
    return {"rhs": rhs, "diag_blocks": diag_blocks, "couple_blocks": couple_blocks, "halo_weight": halo_weight, "neighbours": neighbours, "boundary": boundary}


centre = 4.0
half_width = 2.0

def pick_rows(block, index):
    return block[index]

def apply_operator(rounded, diag32, couple32, halo32, nbrs, bnds):
    values = rounded.astype(jnp.float32)
    high = lax.Precision.HIGHEST
    self_term = jnp.einsum('paij,pajs->pais', diag32, values, precision=high)
    beside = jax.vmap(pick_rows)(values, nbrs)
    cross_term = jnp.einsum('pakij,pakjs->pais', couple32, beside, precision=high)
    flat = values.reshape(N_SPACE, AGG_DEV * EDGE_AGG, values.shape[-1])
    picked = jax.vmap(pick_rows)(flat, bnds)
    empty = jnp.zeros_like(picked[:1, 0])
    from_below = jnp.concatenate([empty, picked[:-1, 1]], 0)
    from_above = jnp.concatenate([picked[1:, 0], empty], 0)
    lower = jnp.einsum('pih,phs->pis', halo32[:, 0], from_below, precision=high)
    upper = jnp.einsum('pih,phs->pis', halo32[:, 1], from_above, precision=high)
    total = self_term + cross_term
    total = total.at[:, 0].add(lower)
    total = total.at[:, AGG_DEV - 1].add(upper)
    return total

def reference(rhs, diag_blocks, couple_blocks, halo_weight, neighbours, boundary):
    diag32 = diag_blocks.astype(jnp.float32).reshape(N_SPACE, AGG_DEV, EDGE_AGG, EDGE_AGG)
    couple32 = couple_blocks.astype(jnp.float32).reshape(N_SPACE, AGG_DEV, NBR, EDGE_AGG, EDGE_AGG)
    halo32 = halo_weight.astype(jnp.float32).reshape(N_SPACE, 2, EDGE_AGG, HALO)
    nbrs = neighbours.reshape(N_SPACE, AGG_DEV, NBR).astype(jnp.int32)
    bnds = boundary.reshape(N_SPACE, 2, HALO).astype(jnp.int32)
    columns = rhs.reshape(EDGES, N_SRC, SRC_DEV).transpose(1, 0, 2)

    def smooth(right):
        shape4 = (N_SPACE, AGG_DEV, EDGE_AGG, SRC_DEV)
        residual = right.reshape(shape4)
        solution = jnp.zeros(shape4, jnp.float32)
        direction = residual / centre
        sigma = centre / half_width
        ratio = 1.0 / sigma
        for sweep in range(SWEEPS):
            solution = solution + direction
            image = apply_operator(direction.astype(jnp.bfloat16), diag32, couple32, halo32, nbrs, bnds)
            residual = residual - image
            if sweep + 1 < SWEEPS:
                ratio_new = 1.0 / (2.0 * sigma - ratio)
                direction = ratio_new * ratio * direction + 2.0 * ratio_new / half_width * residual
                ratio = ratio_new
        squares_res = lax.optimization_barrier(jnp.sum(residual * residual, axis=(0, 1, 2)))
        squares_rhs = lax.optimization_barrier(jnp.sum(right * right, axis=0))
        misfit = jnp.sqrt(squares_res / (squares_rhs + 1e-06))
        return (solution.reshape(EDGES, SRC_DEV), misfit)
    solution, misfit = lax.map(smooth, columns)
    return (solution.transpose(1, 0, 2).reshape(EDGES, SOURCES), misfit.reshape(SOURCES))
```

```python
import functools

import jax
import jax.numpy as jnp
from jax import lax
from jax.experimental import pallas as pl
from jax.experimental.pallas import tpu as pltpu
from jax.sharding import PartitionSpec as P

SWEEPS = 4
CHUNKS = 2
MESH = pl.DeviceIdType.MESH

centre = 4.0
half_width = 2.0


def sweep_weights():
    sigma = centre / half_width
    ratio = 1.0 / sigma
    weights = []
    for _ in range(SWEEPS - 1):
        ratio_new = 1.0 / (2.0 * sigma - ratio)
        weights.append((ratio_new * ratio, 2.0 * ratio_new / half_width))
        ratio = ratio_new
    return weights


def kernel(
    n_space, n_src,
    rhs_ref, diag_ref, couple_ref, halo_ref, nbr_ref, bnd_ref,
    total, misfit_ref,
    res, dirn, rounded, weights, gmat, picks, bounds, outbox, inbox, red_b, red_r,
    rhs_sem, bnd_sem, own_sem, op_send, op_recv, halo_send, halo_recv, sums_send, sums_recv,
):
    me = lax.axis_index("space")
    core = lax.axis_index("src")
    aggs, size, depth = weights.shape
    edges, width = res.shape
    nbrs = couple_ref.shape[1]
    halo = bnd_ref.shape[1]
    part = size // n_src
    cols = width // CHUNKS

    def span(c):
        return pl.ds(c * cols, cols)

    rhs_loads = [
        pltpu.make_async_copy(rhs_ref.at[:, span(c)], res.at[:, span(c)], rhs_sem.at[c])
        for c in range(CHUNKS)
    ]
    bnd_load = pltpu.make_async_copy(bnd_ref, bounds, bnd_sem)
    bnd_load.start()
    for load in rhs_loads:
        load.start()
    rows = pl.ds(pl.multiple_of(core * part, part), part)
    pieces = [(diag_ref, weights.at[:, rows, pl.ds(0, size)])]
    for k in range(nbrs):
        pieces.append((couple_ref.at[:, k], weights.at[:, rows, pl.ds((k + 1) * size, size)]))
    pieces.append((halo_ref, gmat.at[:, rows]))
    own = [pltpu.make_async_copy(a, b, own_sem.at[i]) for i, (a, b) in enumerate(pieces)]
    for load in own:
        load.start()

    barrier = pltpu.get_barrier_semaphore()

    def greet_space(k, carry):
        pl.semaphore_signal(
            barrier, inc=1, device_id={"space": lax.rem(me + k, n_space)}, device_id_type=MESH
        )
        return carry

    lax.fori_loop(1, n_space, greet_space, 0)
    for k in range(1, n_src):
        pl.semaphore_signal(
            barrier, inc=1, device_id={"src": lax.rem(core + k, n_src)}, device_id_type=MESH
        )

    bnd_load.wait()
    at = lax.broadcasted_iota(jnp.int32, (edges, halo), 0)
    for i, side in enumerate((1, 0)):
        hit = (at == bounds[side : side + 1, :]).astype(jnp.float32)
        picks[pl.ds(i * halo, halo), :] = hit.T.astype(jnp.bfloat16)

    @pl.when(me == 0)
    def _():
        inbox[:, :, 0] = jnp.zeros_like(inbox[:, :, 0])

    @pl.when(me == n_space - 1)
    def _():
        inbox[:, :, 1] = jnp.zeros_like(inbox[:, :, 1])

    def pack(s, c):
        picked = jnp.dot(picks[...], rounded[:, :, span(c)].reshape(edges, cols), preferred_element_type=jnp.float32)
        outbox[s, c] = picked.astype(jnp.bfloat16).reshape(2, halo, cols)

    def passed(s, c, side):
        to = lax.rem(me + 1, n_space) if side == 0 else lax.rem(me + n_space - 1, n_space)
        return pltpu.make_async_remote_copy(
            src_ref=outbox.at[s, c, side],
            dst_ref=inbox.at[s, c, side],
            send_sem=halo_send.at[s, c, side],
            recv_sem=halo_recv.at[s, c, side],
            device_id={"space": to},
            device_id_type=MESH,
        )

    sends = (me < n_space - 1, me > 0)
    takes = (me > 0, me < n_space - 1)

    def send(s, c):
        for side in range(2):
            pl.when(sends[side])(passed(s, c, side).start)

    def take(s, c):
        for side in range(2):
            pl.when(takes[side])(passed(s, c, side).wait_recv)

    def share(buffer, index):
        def one(k, carry):
            pltpu.make_async_remote_copy(
                src_ref=buffer.at[me],
                dst_ref=buffer.at[me],
                send_sem=sums_send.at[index],
                recv_sem=sums_recv.at[index],
                device_id={"space": lax.rem(me + k, n_space)},
                device_id_type=MESH,
            ).start()
            return carry

        lax.fori_loop(1, n_space, one, 0)

    def collected(buffer, sem):
        others = buffer.at[pl.ds(0, n_space - 1)]
        pltpu.make_async_copy(others, others, sem).wait()

    for c in range(CHUNKS):
        rhs_loads[c].wait()
        right = res[:, span(c)]
        start = right / centre
        dirn[:, span(c)] = start
        rounded[:, :, span(c)] = start.astype(jnp.bfloat16).reshape(aggs, size, cols)
        pack(0, c)
        if c == 0:
            pl.semaphore_wait(barrier, n_space - 1 + n_src - 1)
        send(0, c)
        red_b[me, :, span(c)] = jnp.sum(right * right, axis=0, keepdims=True)

    moves = []
    for k in range(1, n_src):
        for i, (a, b) in enumerate(pieces):
            move = pltpu.make_async_remote_copy(
                src_ref=a,
                dst_ref=b,
                send_sem=op_send.at[k - 1, i],
                recv_sem=op_recv.at[k - 1, i],
                device_id={"src": lax.rem(core + k, n_src)},
                device_id_type=MESH,
            )
            move.start()
            moves.append(move)
    share(red_b, 0)
    for load in own:
        load.wait()
    for move in moves:
        move.wait()

    def local_part(c):
        for a in range(aggs):
            group = pl.ds(a * size, size)
            beside = [rounded[a, :, span(c)]]
            for k in range(nbrs):
                beside.append(rounded[nbr_ref[k, a], :, span(c)])
            res[group, span(c)] -= jnp.dot(
                weights[a], jnp.concatenate(beside, axis=0), preferred_element_type=jnp.float32
            )

    def halo_part(s, c):
        for side, a in ((0, 0), (1, aggs - 1)):
            group = pl.ds(a * size, size)
            res[group, span(c)] -= jnp.dot(
                gmat[side], inbox[s, c, side], preferred_element_type=jnp.float32
            )

    for c in range(CHUNKS):
        local_part(c)

    steps = sweep_weights()
    for s in range(SWEEPS - 1):
        keep, gain = steps[s]
        for c in range(CHUNKS):
            take(s, c)
            halo_part(s, c)
            before = dirn[:, span(c)]
            after = keep * before + gain * res[:, span(c)]
            rounded[:, :, span(c)] = after.astype(jnp.bfloat16).reshape(aggs, size, cols)
            pack(s + 1, c)
            send(s + 1, c)
            dirn[:, span(c)] = after
            if s == 0:
                total[:, span(c)] = before + after
            else:
                total[:, span(c)] += after
            local_part(c)

    for c in range(CHUNKS):
        take(SWEEPS - 1, c)
        halo_part(SWEEPS - 1, c)
        left = res[:, span(c)]
        red_r[me, :, span(c)] = jnp.sum(left * left, axis=0, keepdims=True)
    share(red_r, 1)
    collected(red_b, sums_recv.at[0])
    bb = jnp.sum(red_b[...], axis=0)
    for s in range(SWEEPS):
        for c in range(CHUNKS):
            for side in range(2):
                pl.when(sends[side])(passed(s, c, side).wait_send)
    collected(red_b, sums_send.at[0])
    collected(red_r, sums_recv.at[1])
    rr = jnp.sum(red_r[...], axis=0)
    misfit_ref[...] = jnp.sqrt(rr / (bb + 1e-06))
    collected(red_r, sums_send.at[1])


def local(n_space, n_src, rhs, diag_blocks, couple_blocks, halo_weight, neighbours, boundary):
    edges, width = rhs.shape
    aggs, part, size = diag_blocks.shape
    nbrs = couple_blocks.shape[1]
    halo = boundary.shape[1]
    cols = width // CHUNKS
    bf16, f32 = jnp.bfloat16, jnp.float32
    dma = pltpu.SemaphoreType.DMA
    outside = pl.BlockSpec(memory_space=pltpu.HBM)
    inside = pl.BlockSpec(memory_space=pltpu.VMEM)
    result, misfit = pl.pallas_call(
        functools.partial(kernel, n_space, n_src),
        out_shape=(
            jax.ShapeDtypeStruct((edges, width), f32),
            jax.ShapeDtypeStruct((1, width), f32),
        ),
        in_specs=[outside] * 4 + [pl.BlockSpec(memory_space=pltpu.SMEM), outside],
        out_specs=(inside, inside),
        scratch_shapes=[
            pltpu.VMEM((edges, width), f32),
            pltpu.VMEM((edges, width), f32),
            pltpu.VMEM((aggs, size, width), bf16),
            pltpu.VMEM((aggs, size, (nbrs + 1) * size), bf16),
            pltpu.VMEM((2, size, halo), bf16),
            pltpu.VMEM((2 * halo, edges), bf16),
            pltpu.VMEM((2, halo), jnp.int32),
            pltpu.VMEM((SWEEPS, CHUNKS, 2, halo, cols), bf16),
            pltpu.VMEM((SWEEPS, CHUNKS, 2, halo, cols), bf16),
            pltpu.VMEM((n_space, 1, width), f32),
            pltpu.VMEM((n_space, 1, width), f32),
            dma((CHUNKS,)),
            dma,
            dma((nbrs + 2,)),
            dma((max(n_src - 1, 1), nbrs + 2)),
            dma((max(n_src - 1, 1), nbrs + 2)),
            dma((SWEEPS, CHUNKS, 2)),
            dma((SWEEPS, CHUNKS, 2)),
            dma((2,)),
            dma((2,)),
        ],
        compiler_params=pltpu.CompilerParams(
            collective_id=0, has_side_effects=True, vmem_limit_bytes=48 * 1024 * 1024
        ),
    )(rhs, diag_blocks, couple_blocks, halo_weight, neighbours.T, boundary)
    return result, misfit.reshape(width)


def solution(mesh):
    placed = (
        P("space", "src"),
        P("space", "src", None),
        P("space", None, "src", None),
        P("space", "src", None),
        P("space", None),
        P("space", None),
    )
    body = functools.partial(local, mesh.shape["space"], mesh.shape["src"])
    return jax.shard_map(
        body, mesh=mesh, in_specs=placed, out_specs=(P("space", "src"), P("src")), check_vma=False
    )
```

```python
import functools

import jax
import jax.numpy as jnp
from jax import lax
from jax.experimental import pallas as pl
from jax.experimental.pallas import tpu as pltpu
from jax.sharding import PartitionSpec as P

SWEEPS = 4
CHUNKS = 4
GROUP = 2
MESH = pl.DeviceIdType.MESH

centre = 4.0
half_width = 2.0


def sweep_weights():
    sigma = centre / half_width
    ratio = 1.0 / sigma
    weights = []
    for _ in range(SWEEPS - 1):
        ratio_new = 1.0 / (2.0 * sigma - ratio)
        weights.append((ratio_new * ratio, 2.0 * ratio_new / half_width))
        ratio = ratio_new
    return weights


def kernel(
    n_space, n_src,
    rhs_ref, diag_ref, couple_ref, halo_ref, nbr_ref, bnd_ref,
    sol_ref, misfit_ref,
    res, dirn, rounded, total, weights, gmat, picks, bounds, outbox, inbox, red_b, red_r,
    rhs_sem, bnd_sem, out_sem, own_sem, op_send, op_recv, halo_send, halo_recv, sums_send, sums_recv, heard,
):
    me = lax.axis_index("space")
    core = lax.axis_index("src")
    aggs, size, depth = weights.shape
    edges, width = res.shape
    nbrs = couple_ref.shape[1]
    halo = bnd_ref.shape[1]
    part = size // n_src
    cols = width // CHUNKS

    def span(c, many=1):
        return pl.ds(c * cols, many * cols)

    rhs_loads = [
        pltpu.make_async_copy(rhs_ref.at[:, span(c)], res.at[:, span(c)], rhs_sem.at[c])
        for c in range(CHUNKS)
    ]
    bnd_load = pltpu.make_async_copy(bnd_ref, bounds, bnd_sem)
    bnd_load.start()
    for load in rhs_loads:
        load.start()
    rows = pl.ds(pl.multiple_of(core * part, part), part)
    pieces = [(diag_ref, weights.at[:, rows, pl.ds(0, size)])]
    for k in range(nbrs):
        pieces.append((couple_ref.at[:, k], weights.at[:, rows, pl.ds((k + 1) * size, size)]))
    pieces.append((halo_ref, gmat.at[:, rows]))
    own = [pltpu.make_async_copy(a, b, own_sem.at[i]) for i, (a, b) in enumerate(pieces)]
    for load in own:
        load.start()

    barrier = pltpu.get_barrier_semaphore()

    def greet(axis, to):
        pl.semaphore_signal(barrier, inc=1, device_id={axis: to}, device_id_type=MESH)

    def across(j):
        return me + (1 - 2 * (lax.div(me, 1 << j) % 2)) * (1 << j)

    rounds = []
    if n_space & (n_space - 1) == 0:
        dims = n_space.bit_length() - 1
        for j in range(dims):
            greet("space", across(j))
        pl.when(me > 0)(lambda: greet("space", me - 1))
        pl.when(me < n_space - 1)(lambda: greet("space", me + 1))
        greeted = dims + (me > 0).astype(jnp.int32) + (me < n_space - 1).astype(jnp.int32)
        rounds = list(range(1, dims))
    else:

        @pl.loop(1, n_space)
        def _(k):
            greet("space", lax.rem(me + k, n_space))

        greeted = n_space - 1
    for k in range(1, n_src):
        greet("src", lax.rem(core + k, n_src))

    def hear(j):
        if j > 1:
            pl.semaphore_wait(heard.at[j - 1], 1)
        pl.semaphore_signal(
            heard.at[j], inc=1, device_id={"space": across(j)}, device_id_type=MESH
        )

    last_round = rounds[-1] if rounds else None

    bnd_load.wait()
    at = lax.broadcasted_iota(jnp.int32, (edges, halo), 0)
    for i, side in enumerate((1, 0)):
        hit = (at == bounds[side : side + 1, :]).astype(jnp.float32)
        picks[pl.ds(i * halo, halo), :] = hit.T.astype(jnp.bfloat16)

    @pl.when(me == 0)
    def _():
        inbox[:, :, 0] = jnp.zeros_like(inbox[:, :, 0])

    @pl.when(me == n_space - 1)
    def _():
        inbox[:, :, 1] = jnp.zeros_like(inbox[:, :, 1])

    def pack(s, c):
        picked = jnp.dot(picks[...], rounded[:, :, span(c)].reshape(edges, cols), preferred_element_type=jnp.float32)
        outbox[s, c] = picked.astype(jnp.bfloat16).reshape(2, halo, cols)

    def passed(s, c, side):
        to = lax.rem(me + 1, n_space) if side == 0 else lax.rem(me + n_space - 1, n_space)
        return pltpu.make_async_remote_copy(
            src_ref=outbox.at[s, c, side],
            dst_ref=inbox.at[s, c, side],
            send_sem=halo_send.at[s, c, side],
            recv_sem=halo_recv.at[s, c, side],
            device_id={"space": to},
            device_id_type=MESH,
        )

    sends = (me < n_space - 1, me > 0)
    takes = (me > 0, me < n_space - 1)

    def send(s, c):
        for side in range(2):
            pl.when(sends[side])(passed(s, c, side).start)

    def take(s, c):
        for side in range(2):
            pl.when(takes[side])(passed(s, c, side).wait_recv)

    def share(buffer, index):
        def one(k, carry):
            pltpu.make_async_remote_copy(
                src_ref=buffer.at[me],
                dst_ref=buffer.at[me],
                send_sem=sums_send.at[index],
                recv_sem=sums_recv.at[index],
                device_id={"space": lax.rem(me + k, n_space)},
                device_id_type=MESH,
            ).start()
            return carry

        lax.fori_loop(1, n_space, one, 0)

    def collected(buffer, sem):
        others = buffer.at[pl.ds(0, n_space - 1)]
        pltpu.make_async_copy(others, others, sem).wait()

    for c in range(CHUNKS):
        rhs_loads[c].wait()
        right = res[:, span(c)]
        start = right / centre
        dirn[:, span(c)] = start
        rounded[:, :, span(c)] = start.astype(jnp.bfloat16).reshape(aggs, size, cols)
        pack(0, c)
        if c == 0:
            pl.semaphore_wait(barrier, greeted + n_src - 1)
        send(0, c)
        red_b[me, :, span(c)] = jnp.sum(right * right, axis=0, keepdims=True)

    moves = []
    for k in range(1, n_src):
        for i, (a, b) in enumerate(pieces):
            move = pltpu.make_async_remote_copy(
                src_ref=a,
                dst_ref=b,
                send_sem=op_send.at[k - 1, i],
                recv_sem=op_recv.at[k - 1, i],
                device_id={"src": lax.rem(core + k, n_src)},
                device_id_type=MESH,
            )
            move.start()
            moves.append(move)
    if rounds:
        hear(rounds.pop(0))
    for load in own:
        load.wait()
    for move in moves:
        move.wait()

    def local_part(c):
        wide = span(c, GROUP)
        for a in range(aggs):
            group = pl.ds(a * size, size)
            beside = [rounded[a, :, wide]]
            for k in range(nbrs):
                beside.append(rounded[nbr_ref[k, a], :, wide])
            res[group, wide] -= jnp.dot(
                weights[a], jnp.concatenate(beside, axis=0), preferred_element_type=jnp.float32
            )

    def halo_part(s, c):
        for side, a in ((0, 0), (1, aggs - 1)):
            group = pl.ds(a * size, size)
            res[group, span(c)] -= jnp.dot(
                gmat[side], inbox[s, c, side], preferred_element_type=jnp.float32
            )

    for c in range(0, CHUNKS, GROUP):
        local_part(c)

    stores = []
    steps = sweep_weights()
    for s in range(SWEEPS - 1):
        keep, gain = steps[s]
        for c in range(CHUNKS):
            take(s, c)
            halo_part(s, c)
            before = dirn[:, span(c)]
            after = keep * before + gain * res[:, span(c)]
            rounded[:, :, span(c)] = after.astype(jnp.bfloat16).reshape(aggs, size, cols)
            pack(s + 1, c)
            send(s + 1, c)
            dirn[:, span(c)] = after
            if s == 0:
                total[:, span(c)] = before + after
            else:
                total[:, span(c)] += after
            if s == SWEEPS - 2:
                store = pltpu.make_async_copy(
                    total.at[:, span(c)], sol_ref.at[:, span(c)], out_sem.at[c]
                )
                store.start()
                stores.append(store)
            if (c + 1) % GROUP == 0:
                local_part(c + 1 - GROUP)
                if rounds:
                    hear(rounds.pop(0))

    assert not rounds
    if last_round is not None:
        pl.semaphore_wait(heard.at[last_round], 1)
    share(red_b, 0)
    for c in range(CHUNKS):
        take(SWEEPS - 1, c)
        halo_part(SWEEPS - 1, c)
        left = res[:, span(c)]
        red_r[me, :, span(c)] = jnp.sum(left * left, axis=0, keepdims=True)
    share(red_r, 1)
    collected(red_b, sums_recv.at[0])
    bb = jnp.sum(red_b[...], axis=0)
    for store in stores:
        store.wait()
    for s in range(SWEEPS):
        for c in range(CHUNKS):
            for side in range(2):
                pl.when(sends[side])(passed(s, c, side).wait_send)
    collected(red_b, sums_send.at[0])
    collected(red_r, sums_recv.at[1])
    rr = jnp.sum(red_r[...], axis=0)
    misfit_ref[...] = jnp.sqrt(rr / (bb + 1e-06))
    collected(red_r, sums_send.at[1])


def local(n_space, n_src, rhs, diag_blocks, couple_blocks, halo_weight, neighbours, boundary):
    edges, width = rhs.shape
    aggs, part, size = diag_blocks.shape
    nbrs = couple_blocks.shape[1]
    halo = boundary.shape[1]
    cols = width // CHUNKS
    bf16, f32 = jnp.bfloat16, jnp.float32
    dma = pltpu.SemaphoreType.DMA
    outside = pl.BlockSpec(memory_space=pltpu.HBM)
    inside = pl.BlockSpec(memory_space=pltpu.VMEM)
    result, misfit = pl.pallas_call(
        functools.partial(kernel, n_space, n_src),
        out_shape=(
            jax.ShapeDtypeStruct((edges, width), f32),
            jax.ShapeDtypeStruct((1, width), f32),
        ),
        in_specs=[outside] * 4 + [pl.BlockSpec(memory_space=pltpu.SMEM), outside],
        out_specs=(outside, inside),
        scratch_shapes=[
            pltpu.VMEM((edges, width), f32),
            pltpu.VMEM((edges, width), f32),
            pltpu.VMEM((aggs, size, width), bf16),
            pltpu.VMEM((edges, width), f32),
            pltpu.VMEM((aggs, size, (nbrs + 1) * size), bf16),
            pltpu.VMEM((2, size, halo), bf16),
            pltpu.VMEM((2 * halo, edges), bf16),
            pltpu.VMEM((2, halo), jnp.int32),
            pltpu.VMEM((SWEEPS, CHUNKS, 2, halo, cols), bf16),
            pltpu.VMEM((SWEEPS, CHUNKS, 2, halo, cols), bf16),
            pltpu.VMEM((n_space, 1, width), f32),
            pltpu.VMEM((n_space, 1, width), f32),
            dma((CHUNKS,)),
            dma,
            dma((CHUNKS,)),
            dma((nbrs + 2,)),
            dma((max(n_src - 1, 1), nbrs + 2)),
            dma((max(n_src - 1, 1), nbrs + 2)),
            dma((SWEEPS, CHUNKS, 2)),
            dma((SWEEPS, CHUNKS, 2)),
            dma((2,)),
            dma((2,)),
            pltpu.SemaphoreType.REGULAR((max(n_space.bit_length() - 1, 1),)),
        ],
        compiler_params=pltpu.CompilerParams(
            collective_id=0, has_side_effects=True, vmem_limit_bytes=67043328
        ),
    )(rhs, diag_blocks, couple_blocks, halo_weight, neighbours.T, boundary)
    return result, misfit.reshape(width)


def solution(mesh):
    placed = (
        P("space", "src"),
        P("space", "src", None),
        P("space", None, "src", None),
        P("space", "src", None),
        P("space", None),
        P("space", None),
    )
    body = functools.partial(local, mesh.shape["space"], mesh.shape["src"])
    return jax.shard_map(
        body, mesh=mesh, in_specs=placed, out_specs=(P("space", "src"), P("src")), check_vma=False
    )
```

```python
import functools

import jax
import jax.numpy as jnp
from jax import lax
from jax.experimental import pallas as pl
from jax.experimental.pallas import tpu as pltpu
from jax.sharding import PartitionSpec as P

SWEEPS = 4
CHUNKS = 4
GROUP = 1
MESH = pl.DeviceIdType.MESH

centre = 4.0
half_width = 2.0


def sweep_weights():
    sigma = centre / half_width
    ratio = 1.0 / sigma
    weights = []
    for _ in range(SWEEPS - 1):
        ratio_new = 1.0 / (2.0 * sigma - ratio)
        weights.append((ratio_new * ratio, 2.0 * ratio_new / half_width))
        ratio = ratio_new
    return weights


def kernel(
    n_space, n_src,
    rhs_ref, diag_ref, couple_ref, halo_ref, nbr_ref, bnd_ref,
    total, misfit_ref,
    res, dirn, rounded, weights, gmat, picks, bounds, outbox, inbox, red_b, red_r,
    rhs_sem, bnd_sem, own_sem, op_send, op_recv, halo_send, halo_recv, sums_send, sums_recv, heard,
):
    me = lax.axis_index("space")
    core = lax.axis_index("src")
    aggs, size, depth = weights.shape
    edges, width = res.shape
    nbrs = couple_ref.shape[1]
    halo = bnd_ref.shape[1]
    part = size // n_src
    cols = width // CHUNKS

    def span(c, many=1):
        return pl.ds(c * cols, many * cols)

    rhs_loads = [
        pltpu.make_async_copy(rhs_ref.at[:, span(c)], res.at[:, span(c)], rhs_sem.at[c])
        for c in range(CHUNKS)
    ]
    bnd_load = pltpu.make_async_copy(bnd_ref, bounds, bnd_sem)
    bnd_load.start()
    for load in rhs_loads:
        load.start()
    rows = pl.ds(pl.multiple_of(core * part, part), part)
    pieces = [(diag_ref, weights.at[:, rows, pl.ds(0, size)])]
    for k in range(nbrs):
        pieces.append((couple_ref.at[:, k], weights.at[:, rows, pl.ds((k + 1) * size, size)]))
    pieces.append((halo_ref, gmat.at[:, rows]))
    own = [pltpu.make_async_copy(a, b, own_sem.at[i]) for i, (a, b) in enumerate(pieces)]
    for load in own:
        load.start()

    barrier = pltpu.get_barrier_semaphore()

    def greet(axis, to):
        pl.semaphore_signal(barrier, inc=1, device_id={axis: to}, device_id_type=MESH)

    def across(j):
        return me + (1 - 2 * (lax.div(me, 1 << j) % 2)) * (1 << j)

    rounds = []
    if n_space & (n_space - 1) == 0:
        dims = n_space.bit_length() - 1
        for j in range(dims):
            greet("space", across(j))
        pl.when(me > 0)(lambda: greet("space", me - 1))
        pl.when(me < n_space - 1)(lambda: greet("space", me + 1))
        greeted = dims + (me > 0).astype(jnp.int32) + (me < n_space - 1).astype(jnp.int32)
        rounds = list(range(1, dims))
    else:

        @pl.loop(1, n_space)
        def _(k):
            greet("space", lax.rem(me + k, n_space))

        greeted = n_space - 1
    for k in range(1, n_src):
        greet("src", lax.rem(core + k, n_src))

    def hear(j):
        if j > 1:
            pl.semaphore_wait(heard.at[j - 1], 1)
        pl.semaphore_signal(
            heard.at[j], inc=1, device_id={"space": across(j)}, device_id_type=MESH
        )

    last_round = rounds[-1] if rounds else None

    bnd_load.wait()
    at = lax.broadcasted_iota(jnp.int32, (edges, halo), 0)
    for i, side in enumerate((1, 0)):
        hit = (at == bounds[side : side + 1, :]).astype(jnp.float32)
        picks[pl.ds(i * halo, halo), :] = hit.T.astype(jnp.bfloat16)

    @pl.when(me == 0)
    def _():
        inbox[:, :, 0] = jnp.zeros_like(inbox[:, :, 0])

    @pl.when(me == n_space - 1)
    def _():
        inbox[:, :, 1] = jnp.zeros_like(inbox[:, :, 1])

    def pack(s, c):
        picked = jnp.dot(picks[...], rounded[:, :, span(c)].reshape(edges, cols), preferred_element_type=jnp.float32)
        outbox[s, c] = picked.astype(jnp.bfloat16).reshape(2, halo, cols)

    def passed(s, c, side):
        to = lax.rem(me + 1, n_space) if side == 0 else lax.rem(me + n_space - 1, n_space)
        return pltpu.make_async_remote_copy(
            src_ref=outbox.at[s, c, side],
            dst_ref=inbox.at[s, c, side],
            send_sem=halo_send.at[s, c, side],
            recv_sem=halo_recv.at[s, c, side],
            device_id={"space": to},
            device_id_type=MESH,
        )

    sends = (me < n_space - 1, me > 0)
    takes = (me > 0, me < n_space - 1)

    def send(s, c):
        for side in range(2):
            pl.when(sends[side])(passed(s, c, side).start)

    def take(s, c):
        for side in range(2):
            pl.when(takes[side])(passed(s, c, side).wait_recv)

    def share(buffer, index):
        def one(k, carry):
            pltpu.make_async_remote_copy(
                src_ref=buffer.at[me],
                dst_ref=buffer.at[me],
                send_sem=sums_send.at[index],
                recv_sem=sums_recv.at[index],
                device_id={"space": lax.rem(me + k, n_space)},
                device_id_type=MESH,
            ).start()
            return carry

        lax.fori_loop(1, n_space, one, 0)

    def collected(buffer, sem):
        others = buffer.at[pl.ds(0, n_space - 1)]
        pltpu.make_async_copy(others, others, sem).wait()

    for c in range(CHUNKS):
        rhs_loads[c].wait()
        right = res[:, span(c)]
        start = right / centre
        dirn[:, span(c)] = start
        rounded[:, :, span(c)] = start.astype(jnp.bfloat16).reshape(aggs, size, cols)
        pack(0, c)
        if c == 0:
            pl.semaphore_wait(barrier, greeted + n_src - 1)
        send(0, c)
        red_b[me, :, span(c)] = jnp.sum(right * right, axis=0, keepdims=True)

    moves = []
    for k in range(1, n_src):
        for i, (a, b) in enumerate(pieces):
            move = pltpu.make_async_remote_copy(
                src_ref=a,
                dst_ref=b,
                send_sem=op_send.at[k - 1, i],
                recv_sem=op_recv.at[k - 1, i],
                device_id={"src": lax.rem(core + k, n_src)},
                device_id_type=MESH,
            )
            move.start()
            moves.append(move)
    if rounds:
        hear(rounds.pop(0))
    for load in own:
        load.wait()
    for move in moves:
        move.wait()

    def local_part(c):
        wide = span(c, GROUP)
        for a in range(aggs):
            group = pl.ds(a * size, size)
            beside = [rounded[a, :, wide]]
            for k in range(nbrs):
                beside.append(rounded[nbr_ref[k, a], :, wide])
            res[group, wide] -= jnp.dot(
                weights[a], jnp.concatenate(beside, axis=0), preferred_element_type=jnp.float32
            )

    def halo_part(s, c):
        for side, a in ((0, 0), (1, aggs - 1)):
            group = pl.ds(a * size, size)
            res[group, span(c)] -= jnp.dot(
                gmat[side], inbox[s, c, side], preferred_element_type=jnp.float32
            )

    for c in range(0, CHUNKS, GROUP):
        local_part(c)

    steps = sweep_weights()
    for s in range(SWEEPS - 1):
        keep, gain = steps[s]
        for c in range(CHUNKS):
            take(s, c)
            halo_part(s, c)
            before = dirn[:, span(c)]
            after = keep * before + gain * res[:, span(c)]
            rounded[:, :, span(c)] = after.astype(jnp.bfloat16).reshape(aggs, size, cols)
            pack(s + 1, c)
            send(s + 1, c)
            dirn[:, span(c)] = after
            if s == 0:
                total[:, span(c)] = before + after
            else:
                total[:, span(c)] += after
            if (c + 1) % GROUP == 0:
                local_part(c + 1 - GROUP)
                if rounds:
                    hear(rounds.pop(0))

    assert not rounds
    if last_round is not None:
        pl.semaphore_wait(heard.at[last_round], 1)
    share(red_b, 0)
    for c in range(CHUNKS):
        take(SWEEPS - 1, c)
        halo_part(SWEEPS - 1, c)
        left = res[:, span(c)]
        red_r[me, :, span(c)] = jnp.sum(left * left, axis=0, keepdims=True)
    share(red_r, 1)
    collected(red_b, sums_recv.at[0])
    bb = jnp.sum(red_b[...], axis=0)
    for s in range(SWEEPS):
        for c in range(CHUNKS):
            for side in range(2):
                pl.when(sends[side])(passed(s, c, side).wait_send)
    collected(red_b, sums_send.at[0])
    collected(red_r, sums_recv.at[1])
    rr = jnp.sum(red_r[...], axis=0)
    misfit_ref[...] = jnp.sqrt(rr / (bb + 1e-06))
    collected(red_r, sums_send.at[1])


def local(n_space, n_src, rhs, diag_blocks, couple_blocks, halo_weight, neighbours, boundary):
    edges, width = rhs.shape
    aggs, part, size = diag_blocks.shape
    nbrs = couple_blocks.shape[1]
    halo = boundary.shape[1]
    cols = width // CHUNKS
    bf16, f32 = jnp.bfloat16, jnp.float32
    dma = pltpu.SemaphoreType.DMA
    outside = pl.BlockSpec(memory_space=pltpu.HBM)
    inside = pl.BlockSpec(memory_space=pltpu.VMEM)
    result, misfit = pl.pallas_call(
        functools.partial(kernel, n_space, n_src),
        out_shape=(
            pltpu.VMEM((edges, width), f32),
            jax.ShapeDtypeStruct((1, width), f32),
        ),
        in_specs=[outside] * 4 + [pl.BlockSpec(memory_space=pltpu.SMEM), outside],
        out_specs=(pl.BlockSpec(memory_space=pltpu.VMEM), inside),
        scratch_shapes=[
            pltpu.VMEM((edges, width), f32),
            pltpu.VMEM((edges, width), f32),
            pltpu.VMEM((aggs, size, width), bf16),
            pltpu.VMEM((aggs, size, (nbrs + 1) * size), bf16),
            pltpu.VMEM((2, size, halo), bf16),
            pltpu.VMEM((2 * halo, edges), bf16),
            pltpu.VMEM((2, halo), jnp.int32),
            pltpu.VMEM((SWEEPS, CHUNKS, 2, halo, cols), bf16),
            pltpu.VMEM((SWEEPS, CHUNKS, 2, halo, cols), bf16),
            pltpu.VMEM((n_space, 1, width), f32),
            pltpu.VMEM((n_space, 1, width), f32),
            dma((CHUNKS,)),
            dma,
            dma((nbrs + 2,)),
            dma((max(n_src - 1, 1), nbrs + 2)),
            dma((max(n_src - 1, 1), nbrs + 2)),
            dma((SWEEPS, CHUNKS, 2)),
            dma((SWEEPS, CHUNKS, 2)),
            dma((2,)),
            dma((2,)),
            pltpu.SemaphoreType.REGULAR((max(n_space.bit_length() - 1, 1),)),
        ],
        compiler_params=pltpu.CompilerParams(
            collective_id=0, has_side_effects=True, vmem_limit_bytes=67043328 - edges * width * 4
        ),
    )(rhs, diag_blocks, couple_blocks, halo_weight, neighbours.T, boundary)
    return result, misfit.reshape(width)


def solution(mesh):
    placed = (
        P("space", "src"),
        P("space", "src", None),
        P("space", None, "src", None),
        P("space", "src", None),
        P("space", None),
        P("space", None),
    )
    body = functools.partial(local, mesh.shape["space"], mesh.shape["src"])
    return jax.shard_map(
        body, mesh=mesh, in_specs=placed, out_specs=(P("space", "src"), P("src")), check_vma=False
    )
```
